256 devices in a mesh: space: 32 (over y, x, core), slot: 8 (over z).
Axes of the slice: x: 4, y: 4, z: 8, core: 2. Of those that a mesh axis runs over, the one named last changes fastest.
Arguments:
- window_values: bfloat16 [65536, 16384], P('space', 'slot'), may hold values from -4 to 4
- window_scales: bfloat16 [512, 16384], P('space', 'slot'), may hold values from 0.049804688 to 1
- slab_values: bfloat16 [65536, 512], P('space', 'slot'), may hold values from -4 to 4
- slab_scales: bfloat16 [512, 512], P('space', 'slot'), may hold values from 0.049804688 to 1
- test_matrix: bfloat16 [16384, 256], P('slot'), may hold values from -1 to 1
- owner_slot: int32 [8], replicated, may hold values from 0 to 7, each once
- offset: int32 [1], replicated, may hold values from 0 to 1536
Outputs:
- pod_basis: bfloat16 [65536, 256], P('space')
- pod_coefs: float32 [256, 16384], P(None, 'slot')
The draws below stay inside these ranges and needn't reach their ends.
All inputs are finite; a program needn't handle non-finite values.
Results may differ from the reference program's by a relative error of at most 0.0049.
Values may be sent and summed in bfloat16 or wider, within the bound.
No kernel may reach another device: no remote copies, remote signals or barrier semaphores. Data moves between devices by JAX's collectives and lax.ppermute only.
A program may use at most 128 MiB of HBM per device.

```python
import math
import jax
import jax.numpy as jnp
from jax import lax

ROWS_DEV = 2048
COLS_DEV = 2048
RANK = 256
SLAB = 512
BLOCK = 128
ROWS = 65536
COLS = 16384
N_SPACE = 32
N_SLOT = 8


def snapshot_values(key, row_count, col_count):
    entries = jax.random.normal(jax.random.fold_in(key, 13), (row_count, col_count), jnp.float32)
    return jnp.clip(entries, -4.0, 4.0).astype(jnp.bfloat16)


def draw_window_values(key, part):
    return snapshot_values(key, ROWS, COLS)


def draw_slab_values(key, part):
    return snapshot_values(key, ROWS, SLAB)


def draw_test_matrix(key, part):
    entries = jnp.clip(jax.random.normal(jax.random.fold_in(key, 22), (COLS, RANK), jnp.float32), -6.0, 6.0)
    return (entries / jnp.sqrt(jnp.float32(COLS))).astype(jnp.bfloat16)


def levels(own_key, shape, cuts, smallest, largest):
    level, own = 1.0, jax.random.fold_in(own_key, 6)
    for position, shards_of in cuts:
        draws = jnp.exp(jax.random.uniform(jax.random.fold_in(own, position), (shards_of,), jnp.float32, smallest / len(cuts), largest / len(cuts)))
        level = level * jnp.repeat(draws, shape[position] // shards_of).reshape([-1 if axis == position else 1 for axis in range(len(shape))])
    return level


def setup_inputs(seed: int = 0) -> dict:
    key_list = jax.random.split(jax.random.key(seed), 8)
    return {
        "window_values": draw_window_values(jax.random.fold_in(key_list[7], 71), 0),
        "window_scales": jnp.clip(jnp.exp(math.log(1.0) - 2.9996462 * jax.random.uniform(key_list[1], (ROWS // BLOCK, COLS), jnp.float32) ** levels(key_list[1], (ROWS // BLOCK, COLS), ((0, 32), (1, 8)), -0.2, 0.2)), 0.049804688, 1.0).astype(jnp.bfloat16),
        "slab_values": draw_slab_values(jax.random.fold_in(key_list[7], 71), 0),
        "slab_scales": jnp.clip(jnp.exp(math.log(1.0) - 2.9996462 * jax.random.uniform(key_list[3], (ROWS // BLOCK, SLAB), jnp.float32) ** levels(key_list[3], (ROWS // BLOCK, SLAB), ((0, 32), (1, 8)), -0.2, 0.2)), 0.049804688, 1.0).astype(jnp.bfloat16),
        "test_matrix": draw_test_matrix(jax.random.fold_in(key_list[7], 71), 0),
        "owner_slot": jax.random.permutation(key_list[5], N_SLOT).astype(jnp.int32),
        "offset": jax.random.randint(key_list[6], (1,), 0, COLS_DEV - SLAB + 1).astype(jnp.int32),
    }


def expand(values, scales):
    row_count, col_count = values.shape
    scaled = values.astype(jnp.float32).reshape(row_count // BLOCK, BLOCK, col_count) * scales.astype(jnp.float32)[:, None, :]
    return scaled.reshape(row_count, col_count).astype(jnp.bfloat16)

def inverse_factor(gram_matrix):
    lower_factor = jnp.linalg.cholesky(gram_matrix)
    identity = jnp.eye(gram_matrix.shape[0], dtype=jnp.float32)
    return lax.linalg.triangular_solve(lower_factor, identity, left_side=True, lower=True)

def reference(window_values, window_scales, slab_values, slab_scales, test_matrix, owner_slot, offset):
    first_col = (owner_slot[0] * COLS_DEV + offset[0]).astype(jnp.int32)
    values = lax.dynamic_update_slice(window_values, slab_values, (jnp.int32(0), first_col))
    scales = lax.dynamic_update_slice(window_scales, slab_scales, (jnp.int32(0), first_col))
    value_blocks = values.reshape(N_SPACE, ROWS_DEV, COLS)
    scale_blocks = scales.reshape(N_SPACE, ROWS_DEV // BLOCK, COLS)

    def sketch_block(blocks):
        return jnp.dot(expand(blocks[0], blocks[1]).astype(jnp.float32), test_matrix.astype(jnp.float32), preferred_element_type=jnp.float32)
    sketch = lax.map(sketch_block, (value_blocks, scale_blocks))
    flat_sketch = sketch.reshape(ROWS, RANK)
    gram_matrix = jnp.dot(flat_sketch.T.astype(jnp.float32), flat_sketch.astype(jnp.float32), precision=lax.Precision.HIGHEST, preferred_element_type=jnp.float32) / ROWS
    inverse = inverse_factor(gram_matrix)
    pod_basis = jnp.dot(flat_sketch.astype(jnp.float32), inverse.T.astype(jnp.float32), precision=lax.Precision.HIGHEST, preferred_element_type=jnp.float32).astype(jnp.bfloat16)

    def cross_block(accum_sum, blocks):
        window = expand(blocks[0], blocks[1]).astype(jnp.float32)
        partial_value = lax.dot_general(blocks[2].astype(jnp.float32), window.astype(jnp.float32), (((0,), (0,)), ((), ())), precision=lax.Precision.HIGHEST, preferred_element_type=jnp.float32)
        return (accum_sum + partial_value, None)
    cross, _ = lax.scan(cross_block, jnp.zeros((RANK, COLS), jnp.float32), (value_blocks, scale_blocks, sketch))
    pod_coefs = jnp.dot(inverse.astype(jnp.float32), cross.astype(jnp.float32), precision=lax.Precision.HIGHEST, preferred_element_type=jnp.float32)
    return (pod_basis, pod_coefs / jnp.sqrt(jnp.float32(ROWS)))
```

```python
import functools

import jax
import jax.numpy as jnp
from jax import lax
from jax.experimental import pallas as pl
from jax.experimental.pallas import tpu as pltpu
from jax.sharding import PartitionSpec as P

SLAB = 512
BLOCK = 128
F32, BF16 = jnp.float32, jnp.bfloat16
HIGHEST = lax.Precision.HIGHEST

CORES = 2


def space_shift(dy, dx, dc=0):
    index = lambda y, x, c: (y % 4) * 8 + (x % 4) * 2 + c
    return [
        (index(y, x, c), index(y + dy, x + dx, (c + dc) % 2))
        for y in range(4)
        for x in range(4)
        for c in range(2)
    ]


def ring(value, distance, size):
    return lax.ppermute(value, "slot", [(i, (i + distance) % size) for i in range(size)])


def along(value, dy, dx, dc=0):
    return lax.ppermute(value, "space", space_shift(dy, dx, dc))


def contract(left, right, left_dim, right_dim, precision=None):
    return lax.dot_general(
        left,
        right,
        (((left_dim,), (right_dim,)), ((), ())),
        precision=precision,
        preferred_element_type=F32,
    )


def split(value):
    high = value.astype(BF16)
    return high, (value - high.astype(F32)).astype(BF16)


VMEM = pl.BlockSpec(memory_space=pltpu.VMEM)


def expand_block(values_ref, scale_ref, block, row_blocks):
    return jnp.concatenate(
        [
            values_ref[BLOCK * h : BLOCK * (h + 1), :]
            * scale_ref[pl.ds(block * row_blocks + h, 1), :].astype(BF16)
            for h in range(row_blocks)
        ],
        axis=0,
    )


def sketch_kernel(meta, values_ref, scales_ref, test_ref, out_ref, scale_ref):
    step, parts = pl.program_id(0), pl.num_programs(0)
    block = lax.rem(meta[0] + step, parts)

    @pl.when(step == 0)
    def _():
        columns = lax.broadcasted_iota(jnp.int32, scales_ref.shape, 1)
        evicted = (columns >= meta[2]) & (columns < meta[2] + SLAB)
        scale_ref[...] = jnp.where(evicted, 0.0, scales_ref[...].astype(F32))

    rows = values_ref.shape[0]
    window = expand_block(values_ref, scale_ref, block, rows // BLOCK)
    out_ref[...] = jnp.dot(window, test_ref[...], preferred_element_type=F32)


def sketch_window(meta, values, scales, test, parts):
    rows, cols = values.shape
    rank = test.shape[1]
    return pl.pallas_call(
        sketch_kernel,
        grid_spec=pltpu.PrefetchScalarGridSpec(
            num_scalar_prefetch=1,
            grid=(parts,),
            in_specs=[
                pl.BlockSpec((rows // parts, cols), lambda i, m: (lax.rem(m[0] + i, parts), 0)),
                pl.BlockSpec(scales.shape, lambda i, m: (0, 0)),
                pl.BlockSpec(test.shape, lambda i, m: (0, 0)),
            ],
            out_specs=pl.BlockSpec((rows // parts, rank), lambda i, m: (i, 0)),
            scratch_shapes=[pltpu.VMEM(scales.shape, F32)],
        ),
        out_shape=jax.ShapeDtypeStruct((rows, rank), F32),
        name="sketch_window",
    )(meta, values, scales, test)


def slab_kernel(parts, meta, partial_ref, slab_ref, scales_ref, tests_ref, *refs):
    out_refs, scale_ref = refs[:-1], refs[-1]
    rows = partial_ref.shape[0] // parts
    scale_ref[...] = scales_ref[...].astype(F32)
    test = tests_ref[meta[3]]
    for k in range(parts):
        block = lax.rem(meta[0] + k, parts)
        values = slab_ref.at[pl.ds(pl.multiple_of(block * rows, rows), rows), :]
        slab = expand_block(values, scale_ref, block, rows // BLOCK)
        total = partial_ref[rows * k : rows * (k + 1), :] + jnp.dot(
            slab, test, preferred_element_type=F32
        )
        out_refs[k][...] = total.astype(BF16)


def add_slab(meta, partial, slab, scales, tests, parts):
    rows, rank = partial.shape
    return pl.pallas_call(
        functools.partial(slab_kernel, parts),
        in_specs=[pl.BlockSpec(memory_space=pltpu.SMEM)] + [VMEM] * 4,
        out_specs=[VMEM] * parts,
        out_shape=[jax.ShapeDtypeStruct((rows // parts, rank), BF16)] * parts,
        scratch_shapes=[pltpu.VMEM(scales.shape, F32)],
        name="add_slab",
    )(meta, partial, slab, scales, tests)


def cross_kernel(parts, meta, values_ref, scales_ref, slab_ref, slab_scales_ref, *refs):
    sketch_refs = refs[:parts]
    mine_ref, theirs_ref, gram_mine_ref, gram_theirs_ref = refs[parts : parts + 4]
    block_ref, cross_ref, gram_ref, new_ref, scale_ref, slab_scale_ref = refs[parts + 4 :]
    step = pl.program_id(0)
    distance = lax.rem(step - meta[0] + parts, parts)
    for k in range(parts):

        @pl.when(distance == k)
        def _(k=k):
            block_ref[...] = sketch_refs[k][...]

    @pl.when(step == 0)
    def _():
        scale_ref[...] = scales_ref[...].astype(F32)
        slab_scale_ref[...] = slab_scales_ref[...].astype(F32)

    rows = values_ref.shape[0]
    sketch = block_ref[...]
    window = expand_block(values_ref, scale_ref, step, rows // BLOCK)
    slab = expand_block(slab_ref, slab_scale_ref, step, rows // BLOCK)
    cross = contract(sketch, window, 0, 0)
    gram = contract(sketch, sketch, 0, 0)
    new = contract(slab, sketch, 0, 0)

    @pl.when(step == 0)
    def _():
        cross_ref[...] = cross
        gram_ref[...] = gram
        new_ref[...] = new

    @pl.when(step > 0)
    def _():
        cross_ref[...] += cross
        gram_ref[...] += gram
        new_ref[...] += new

    @pl.when(step == parts - 1)
    def _():
        core = meta[1]
        half, new_half = cross_ref.shape[0] // CORES, new_ref.shape[0] // CORES
        for out, gram_out, which in (
            (mine_ref, gram_mine_ref, core),
            (theirs_ref, gram_theirs_ref, 1 - core),
        ):
            lines = pl.ds(pl.multiple_of(which * half, half), half)
            out[...] = cross_ref[lines, :].astype(BF16)
            gram_out[:half, :] = gram_ref[lines, :]
            gram_out[half:, :] = new_ref[
                pl.ds(pl.multiple_of(which * new_half, new_half), new_half), :
            ]


def products(meta, values, scales, slab, slab_scales, sketch_blocks):
    parts = len(sketch_blocks)
    rows, cols = values.shape
    rank = sketch_blocks[0].shape[1]
    fixed = lambda shape: pl.BlockSpec(shape, lambda i, m: (0, 0))
    half, width = rank // CORES, slab.shape[1]
    lines = half + width // CORES
    return pl.pallas_call(
        functools.partial(cross_kernel, parts),
        grid_spec=pltpu.PrefetchScalarGridSpec(
            num_scalar_prefetch=1,
            grid=(parts,),
            in_specs=[
                pl.BlockSpec((rows // parts, cols), lambda i, m: (i, 0)),
                fixed(scales.shape),
                pl.BlockSpec((rows // parts, width), lambda i, m: (i, 0)),
                fixed(slab_scales.shape),
            ]
            + [fixed((rows // parts, rank))] * parts,
            out_specs=[fixed((half, cols))] * 2 + [fixed((lines, rank))] * 2,
            scratch_shapes=[
                pltpu.VMEM((rows // parts, rank), BF16),
                pltpu.VMEM((rank, cols), F32),
                pltpu.VMEM((rank, rank), F32),
                pltpu.VMEM((width, rank), F32),
                pltpu.VMEM(scales.shape, F32),
                pltpu.VMEM(slab_scales.shape, F32),
            ],
        ),
        out_shape=[jax.ShapeDtypeStruct((half, cols), BF16)] * 2
        + [jax.ShapeDtypeStruct((lines, rank), F32)] * 2,
        name="products",
    )(meta, values, scales, slab, slab_scales, *sketch_blocks)


def sublane(value, row):
    return jnp.broadcast_to(value[row : row + 1, :], value.shape)


def lane(value, col):
    return jnp.broadcast_to(value[:, col : col + 1], value.shape)


def inverse_factor(matrix):
    size = matrix.shape[0]
    groups = size // 8
    cols = lax.broadcasted_iota(jnp.int32, (8, size), 1)
    rows = lax.broadcasted_iota(jnp.int32, (8, size), 0)
    a = [matrix[8 * g : 8 * g + 8, :] for g in range(groups)]
    m = [jnp.where(cols == rows + 8 * g, 1.0, 0.0).astype(F32) for g in range(groups)]
    for g in range(groups):
        pivot = [lane(a[g], 8 * g + c) for c in range(8)]
        below = {h: [lane(a[h], 8 * g + c) for c in range(8)] for h in range(g + 1, groups)}
        for c in range(8):
            reciprocal = 1.0 / sublane(pivot[c], c)
            a_row, m_row = sublane(a[g], c), sublane(m[g], c)
            pivots = [sublane(pivot[k], c) for k in range(8)]
            if c < 7:
                factor = jnp.where(rows > c, pivot[c] * reciprocal, 0.0)
                a[g] = a[g] - factor * a_row
                m[g] = m[g] - factor * m_row
                for k in range(c + 1, 8):
                    pivot[k] = pivot[k] - factor * pivots[k]
            for h in range(g + 1, groups):
                factor = below[h][c] * reciprocal
                a[h] = a[h] - factor * a_row
                m[h] = m[h] - factor * m_row
                for k in range(c + 1, 8):
                    below[h][k] = below[h][k] - factor * pivots[k]
    out = []
    for g in range(groups):
        diagonal = jnp.sum(jnp.where(cols == rows + 8 * g, a[g], 0.0), axis=1, keepdims=True)
        out.append(m[g] * lax.rsqrt(diagonal))
    return jnp.concatenate(out, axis=0)


def factor_kernel(row_total, meta, mine_ref, other_ref, out_ref, gram_ref):
    half = out_ref.shape[0] // 2
    core = meta[1]
    gram_ref[pl.ds(pl.multiple_of(core * half, half), half), :] = mine_ref[:half, :]
    gram_ref[pl.ds(pl.multiple_of((1 - core) * half, half), half), :] = other_ref[:half, :]
    gram = gram_ref[...] * (1.0 / row_total)
    first = inverse_factor(gram[:half, :half])
    upper = contract(first, gram[:half, half:], 1, 0, HIGHEST)
    rest = gram[half:, half:] - contract(upper, upper, 0, 0, HIGHEST)
    below = -contract(upper, first, 0, 0, HIGHEST)
    second = inverse_factor(rest)
    out_ref[:half, :half] = first
    out_ref[:half, half:] = jnp.zeros((half, half), F32)
    out_ref[half:, :half] = contract(second, below, 1, 0, HIGHEST)
    out_ref[half:, half:] = second


def invert(meta, mine, other, row_total):
    rank = mine.shape[1]
    return pl.pallas_call(
        functools.partial(factor_kernel, row_total),
        in_specs=[pl.BlockSpec(memory_space=pltpu.SMEM), VMEM, VMEM],
        out_specs=VMEM,
        out_shape=jax.ShapeDtypeStruct((rank, rank), F32),
        scratch_shapes=[pltpu.VMEM((rank, rank), F32)],
        name="invert",
    )(meta, mine, other)


def basis_kernel(parts, meta, inverse_ref, *refs):
    sketch_refs, out_ref = refs[:parts], refs[parts]
    rows = sketch_refs[0].shape[0]
    high, low = split(inverse_ref[...])
    for k in range(parts):
        block = lax.rem(meta[0] + k, parts)
        sketch = sketch_refs[k][...]
        out_ref[pl.ds(pl.multiple_of(block * rows, rows), rows), :] = (
            contract(sketch, high, 1, 1) + contract(sketch, low, 1, 1)
        ).astype(BF16)


def basis(meta, inverse, sketch_blocks):
    rows, rank = sketch_blocks[0].shape
    parts = len(sketch_blocks)
    return pl.pallas_call(
        functools.partial(basis_kernel, parts),
        in_specs=[pl.BlockSpec(memory_space=pltpu.SMEM)] + [VMEM] * (parts + 1),
        out_specs=VMEM,
        out_shape=jax.ShapeDtypeStruct((rows * parts, rank), BF16),
        name="basis",
    )(meta, inverse, *sketch_blocks)


def place_kernel(meta, slabs_ref, out_ref):
    cols = lax.broadcasted_iota(jnp.int32, (SLAB, out_ref.shape[1]), 1)
    rows = lax.broadcasted_iota(jnp.int32, (SLAB, out_ref.shape[1]), 0)
    selection = jnp.where(cols == rows + meta[2], 1.0, 0.0).astype(BF16)
    out_ref[...] = contract(slabs_ref[...], selection, 0, 0).astype(BF16)


def place(meta, slabs, cols):
    return pl.pallas_call(
        place_kernel,
        in_specs=[pl.BlockSpec(memory_space=pltpu.SMEM), VMEM],
        out_specs=VMEM,
        out_shape=jax.ShapeDtypeStruct((slabs.shape[1], cols), BF16),
        name="place",
    )(meta, slabs)


def coefs_kernel(scale, meta, inverse_ref, mine_ref, other_ref, placed_ref, out_ref, cross_ref):
    half = mine_ref.shape[0]
    cols = lax.broadcasted_iota(jnp.int32, mine_ref.shape, 1)
    evicted = (cols >= meta[2]) & (cols < meta[2] + SLAB)
    for ref, core in ((mine_ref, meta[1]), (other_ref, 1 - meta[1])):
        lines = pl.ds(pl.multiple_of(core * half, half), half)
        cross_ref[lines, :] = jnp.where(evicted, placed_ref[lines, :], ref[...])
    high, low = split(inverse_ref[...] * scale)
    cross = cross_ref[...]
    out_ref[...] = contract(high, cross, 1, 0) + contract(low, cross, 1, 0)


def coefs(meta, inverse, mine, other, placed, scale):
    return pl.pallas_call(
        functools.partial(coefs_kernel, scale),
        in_specs=[pl.BlockSpec(memory_space=pltpu.SMEM)] + [VMEM] * 4,
        out_specs=VMEM,
        out_shape=jax.ShapeDtypeStruct(placed.shape, F32),
        scratch_shapes=[pltpu.VMEM(placed.shape, BF16)],
        name="coefs",
    )(meta, inverse, mine, other, placed)


def swap_all(value, devices, axis, groups=None):
    return lax.all_to_all(
        jnp.broadcast_to(value[None], (devices, *value.shape)),
        axis,
        0,
        0,
        axis_index_groups=groups,
        tiled=True,
    )


def local(window_values, window_scales, slab_values, slab_scales, test_matrix, owner_slot, offset):
    rows, cols = window_values.shape
    rank = test_matrix.shape[1]
    width = slab_values.shape[1]
    slots, spaces = lax.axis_size("slot"), lax.axis_size("space")
    chips = spaces // CORES
    same_core = [[CORES * i + c for i in range(chips)] for c in range(CORES)]
    row_total = rows * spaces
    slot, core = lax.axis_index("slot"), lax.rem(lax.axis_index("space"), CORES)
    owner, first = owner_slot[0], offset[0]
    where = jnp.arange(4)
    meta = jnp.where(
        where == 0,
        slot,
        jnp.where(
            where == 1,
            core,
            jnp.where(where == 2, jnp.where(slot == owner, first, 2 * cols), owner),
        ),
    ).astype(jnp.int32)

    test_rows = lax.dynamic_slice_in_dim(test_matrix, first, SLAB, 0)
    tests = lax.all_to_all(test_rows.reshape(slots, width, rank), "slot", 0, 0, tiled=True)
    partial = sketch_window(meta, window_values, window_scales, test_matrix, slots)
    blocks = add_slab(meta, partial, slab_values, slab_scales, tests, slots)

    received = [ring(blocks[k], k, slots) for k in (4, 3, 5, 2, 6, 1, 7)]
    own = blocks[0].astype(F32)
    for piece in received:
        own = own + piece.astype(F32)
    own = own.astype(BF16)

    right, left = ring(own, 1, slots), ring(own, -1, slots)
    right3, left3 = ring(own, 3, slots), ring(own, -3, slots)
    right2, left2, right4 = ring(right, 1, slots), ring(left, -1, slots), ring(right, 3, slots)
    sketch_blocks = [own, left, left2, left3, right4, right3, right2, right]

    mine, theirs, gram_mine, gram_theirs = products(
        meta, window_values, window_scales, slab_values, slab_scales, sketch_blocks
    )

    gram = gram_mine + along(gram_theirs, 0, 0, 1)
    for dy, dx in ((0, 1), (1, 0)):
        far, near, back = (along(gram, dy * d, dx * d) for d in (2, 1, 3))
        gram = (gram + far) + (near + back)
    gram_other = along(gram, 0, 0, 1)

    half = (mine.astype(F32) + along(theirs, 0, 0, 1).astype(F32)).astype(BF16)
    lines = rank // spaces
    pieces = lax.all_to_all(
        half.reshape(chips, lines, cols), "space", 0, 0, axis_index_groups=same_core, tiled=True
    )
    total = jnp.sum(pieces.astype(F32), axis=0).astype(BF16)
    cross_mine = swap_all(total, chips, "space", same_core).reshape(rank // CORES, cols)
    cross_other = along(cross_mine, 0, 0, 1)

    inverse = invert(meta, gram, gram_other, row_total)
    new_mine, new_other = gram[rank // CORES :], gram_other[rank // CORES :]
    new = jnp.where(
        core == 0,
        jnp.concatenate([new_mine, new_other], 0),
        jnp.concatenate([new_other, new_mine], 0),
    ).astype(BF16)
    slabs = swap_all(new, slots, "slot").reshape(SLAB, rank)
    pod_basis = basis(meta, inverse, sketch_blocks)
    placed = place(meta, slabs, cols)
    pod_coefs = coefs(
        meta, inverse, cross_mine, cross_other, placed, 1.0 / float(row_total) ** 0.5
    )
    return pod_basis, pod_coefs


def solution(mesh):
    return jax.shard_map(
        local,
        mesh=mesh,
        in_specs=(
            P("space", "slot"),
            P("space", "slot"),
            P("space", "slot"),
            P("space", "slot"),
            P("slot", None),
            P(),
            P(),
        ),
        out_specs=(P("space", None), P(None, "slot")),
        check_vma=False,
    )
```

```python
import functools

import jax
import jax.numpy as jnp
from jax import lax
from jax.experimental import pallas as pl
from jax.experimental.pallas import tpu as pltpu
from jax.sharding import PartitionSpec as P


SLAB = 512
BLOCK = 128
F32, BF16 = jnp.float32, jnp.bfloat16
HIGHEST = lax.Precision.HIGHEST

CORES = 2


def space_shift(dy, dx, dc=0):
    index = lambda y, x, c: (y % 4) * 8 + (x % 4) * 2 + c
    return [
        (index(y, x, c), index(y + dy, x + dx, (c + dc) % 2))
        for y in range(4)
        for x in range(4)
        for c in range(2)
    ]


def ring(value, distance, size):
    return lax.ppermute(value, "slot", [(i, (i + distance) % size) for i in range(size)])


def along(value, dy, dx, dc=0):
    return lax.ppermute(value, "space", space_shift(dy, dx, dc))


def contract(left, right, left_dim, right_dim, precision=None):
    return lax.dot_general(
        left,
        right,
        (((left_dim,), (right_dim,)), ((), ())),
        precision=precision,
        preferred_element_type=F32,
    )


def split(value):
    high = value.astype(BF16)
    return high, (value - high.astype(F32)).astype(BF16)


VMEM = pl.BlockSpec(memory_space=pltpu.VMEM)
SMEM = pl.BlockSpec(memory_space=pltpu.SMEM)


def expand(values_ref, scale_ref, first, count):
    return jnp.concatenate(
        [
            values_ref[BLOCK * b : BLOCK * (b + 1), :] * scale_ref[b : b + 1, :].astype(BF16)
            for b in range(first, first + count)
        ],
        axis=0,
    )


def expand_slab(slab_ref, scale_ref, row_blocks):
    return jnp.concatenate(
        [
            slab_ref[:, BLOCK * b : BLOCK * (b + 1)] * scale_ref[:, b : b + 1].astype(BF16)
            for b in range(row_blocks)
        ],
        axis=1,
    )


def sketch_kernel(meta, values_ref, scales_ref, test_ref, out_ref, scale_ref):
    columns = lax.broadcasted_iota(jnp.int32, scales_ref.shape, 1)
    evicted = (columns >= meta[2]) & (columns < meta[2] + SLAB)
    scale_ref[...] = jnp.where(evicted, 0.0, scales_ref[...].astype(F32))
    row_blocks = scales_ref.shape[0]
    count = row_blocks // 4
    for first in range(0, row_blocks, count):
        window = expand(values_ref, scale_ref, first, count)
        out_ref[BLOCK * first : BLOCK * (first + count), :] = jnp.dot(
            window, test_ref[...], preferred_element_type=F32
        )


def sketch_window(meta, values, scales, test):
    return pl.pallas_call(
        sketch_kernel,
        in_specs=[SMEM] + [VMEM] * 3,
        out_specs=VMEM,
        out_shape=jax.ShapeDtypeStruct((values.shape[0], test.shape[1]), F32),
        scratch_shapes=[pltpu.VMEM(scales.shape, F32)],
        compiler_params=pltpu.CompilerParams(vmem_limit_bytes=40 * 2**20),
        name="sketch_window",
    )(meta, values, scales, test)


def slab_kernel(parts, meta, partial_ref, slab_ref, scales_ref, tests_ref, *refs):
    out_refs, sum_ref, scale_ref = refs[:-2], refs[-2], refs[-1]
    rows = partial_ref.shape[0] // parts
    scale_ref[...] = scales_ref[...].astype(F32)
    slab = expand_slab(slab_ref, scale_ref, partial_ref.shape[0] // BLOCK)
    sum_ref[...] = (partial_ref[...] + contract(slab, tests_ref[meta[3]], 0, 0)).astype(BF16)
    pieces = []
    for k in range(parts):
        whole = (k, 0, rows)
        pieces += [(k, 0, rows // 2), (k, rows // 2, rows)] if 2 * k == parts else [whole]
    for out_ref, (k, start, stop) in zip(out_refs, pieces):
        block = pl.multiple_of(lax.rem(meta[0] + k, parts) * rows + start, rows // 2)
        out_ref[...] = sum_ref[pl.ds(block, stop - start), :]


def add_slab(meta, partial, slab, scales, tests, parts):
    rows, rank = partial.shape
    sizes = [rows // parts] * (parts // 2) + [rows // parts // 2] * 2
    sizes += [rows // parts] * (parts // 2 - 1)
    return pl.pallas_call(
        functools.partial(slab_kernel, parts),
        in_specs=[SMEM] + [VMEM] * 4,
        out_specs=[VMEM] * len(sizes),
        out_shape=[jax.ShapeDtypeStruct((size, rank), BF16) for size in sizes],
        scratch_shapes=[pltpu.VMEM(partial.shape, BF16), pltpu.VMEM(scales.shape, F32)],
        compiler_params=pltpu.CompilerParams(vmem_limit_bytes=40 * 2**20),
        name="add_slab",
    )(meta, partial, slab, scales, tests)


def gather_blocks(parts, meta, sketch_refs, out_ref):
    rows = out_ref.shape[0] // parts
    start = 0
    for ref in sketch_refs:
        k, inside = divmod(start, rows)
        line = pl.multiple_of(lax.rem(meta[0] + k, parts) * rows + inside, rows // 2)
        out_ref[pl.ds(line, ref.shape[0]), :] = ref[...]
        start += ref.shape[0]


def cross_kernel(parts, meta, values_ref, scales_ref, slab_ref, slab_scales_ref, *refs):
    sketch_refs, refs = refs[:-9], refs[-9:]
    mine_ref, theirs_ref, gram_mine_ref, gram_theirs_ref, sketch_ref = refs[:5]
    cross_ref, gram_ref, scale_ref, slab_scale_ref = refs[5:]
    gather_blocks(parts, meta, sketch_refs, sketch_ref)
    scale_ref[...] = scales_ref[...].astype(F32)
    slab_scale_ref[...] = slab_scales_ref[...].astype(F32)
    rank, row_blocks = sketch_ref.shape[1], scales_ref.shape[0]
    width, cols = slab_ref.shape[0], values_ref.shape[1]
    sketch = sketch_ref[...]
    gram = contract(sketch, sketch, 0, 0)
    half, eighth = rank // 2, rank // 8
    for c in range(CORES):
        block = gram[half * c : half * (c + 1), half * c : half * (c + 1)]
        below = gram[half + 2 * eighth * c : half + 2 * eighth * (c + 1), :half]
        gram_ref[c, : half // 2, :half] = block[: half // 2]
        gram_ref[c, : half // 2, half:] = block[half // 2 :]
        gram_ref[c, half // 2 :, :half] = below[:eighth]
        gram_ref[c, half // 2 :, half:] = below[eighth:]
    slab = expand_slab(slab_ref, slab_scale_ref, row_blocks)
    cross_ref[:, cols:] = jnp.zeros((rank, cross_ref.shape[1] - cols), F32)
    cross_ref[:, cols : cols + width] = contract(sketch, slab, 0, 1)
    count = row_blocks // 2
    for first in range(0, row_blocks, count):
        window = expand(values_ref, scale_ref, first, count)
        part = contract(sketch[BLOCK * first : BLOCK * (first + count), :], window, 0, 0)
        cross_ref[:, :cols] = part if first == 0 else cross_ref[:, :cols] + part
    core = meta[1]
    for out, gram_out, which in (
        (mine_ref, gram_mine_ref, core),
        (theirs_ref, gram_theirs_ref, 1 - core),
    ):
        lines = pl.ds(pl.multiple_of(which * half, half), half)
        out[...] = cross_ref[lines, :].astype(BF16)
        gram_out[...] = gram_ref[which]


def products(meta, values, scales, slab, slab_scales, sketch_blocks, parts):
    rows, cols = values.shape
    rank = sketch_blocks[0].shape[1]
    half, lanes = rank // CORES, cols + 128
    gram_half = (3 * rank // 8, rank)
    return pl.pallas_call(
        functools.partial(cross_kernel, parts),
        in_specs=[SMEM] + [VMEM] * (4 + len(sketch_blocks)),
        out_specs=[VMEM] * 5,
        out_shape=[jax.ShapeDtypeStruct((half, lanes), BF16)] * 2
        + [jax.ShapeDtypeStruct(gram_half, F32)] * 2
        + [jax.ShapeDtypeStruct((rows, rank), BF16)],
        scratch_shapes=[
            pltpu.VMEM((rank, lanes), F32),
            pltpu.VMEM((CORES, *gram_half), F32),
            pltpu.VMEM(scales.shape, F32),
            pltpu.VMEM(slab_scales.shape, F32),
        ],
        compiler_params=pltpu.CompilerParams(vmem_limit_bytes=40 * 2**20),
        name="products",
    )(meta, values, scales, slab, slab_scales, *sketch_blocks)


def pair_kernel(mine_ref, other_ref, out_ref):
    lines = out_ref.shape[1]
    total = mine_ref[...].astype(F32) + other_ref[...].astype(F32)
    for chip in range(out_ref.shape[0]):
        out_ref[chip] = total[lines * chip : lines * (chip + 1), :].astype(BF16)


def add_pair(mine, other, chips):
    rows, lanes = mine.shape
    return pl.pallas_call(
        pair_kernel,
        in_specs=[VMEM] * 2,
        out_specs=VMEM,
        out_shape=jax.ShapeDtypeStruct((chips, rows // chips, lanes), BF16),
        compiler_params=pltpu.CompilerParams(vmem_limit_bytes=40 * 2**20),
        name="add_pair",
    )(mine, other)


def sum_kernel(pieces_ref, cross_ref, new_ref):
    cols = cross_ref.shape[1]
    total = pieces_ref[0].astype(F32)
    for chip in range(1, pieces_ref.shape[0]):
        total += pieces_ref[chip].astype(F32)
    cross_ref[...] = total[:, :cols]
    new = total[:, cols:].astype(BF16)
    for slot in range(new_ref.shape[0]):
        new_ref[slot] = new


def sum_pieces(pieces, cols, slots):
    _, lines, lanes = pieces.shape
    return pl.pallas_call(
        sum_kernel,
        in_specs=[VMEM],
        out_specs=[VMEM] * 2,
        out_shape=[
            jax.ShapeDtypeStruct((lines, cols), F32),
            jax.ShapeDtypeStruct((slots, lines, lanes - cols), BF16),
        ],
        compiler_params=pltpu.CompilerParams(vmem_limit_bytes=40 * 2**20),
        name="sum_pieces",
    )(pieces)


def insert_kernel(width, meta, cross_ref, slabs_ref, out_ref, line_ref):
    lines, cols = cross_ref.shape
    line_ref[:, :cols] = cross_ref[...]

    @pl.when(meta[2] < cols)
    def _():
        slots, _, lanes = slabs_ref.shape
        inside = lax.rem(meta[2], 128)
        window = pl.ds(pl.multiple_of(meta[2] - inside, 128), SLAB + 128)
        column = lax.broadcasted_iota(jnp.int32, (lanes, SLAB + 128), 1)
        row = lax.broadcasted_iota(jnp.int32, (lanes, SLAB + 128), 0)
        placed = jnp.zeros((lines, SLAB + 128), F32)
        for slot in range(slots):
            hit = (column == row + (inside + width * slot)) & (row < width)
            selection = jnp.where(hit, 1.0, 0.0).astype(BF16)
            placed += contract(slabs_ref[slot], selection, 1, 0)
        column = lax.broadcasted_iota(jnp.int32, placed.shape, 1)
        replaced = (column >= inside) & (column < inside + SLAB)
        line_ref[:, window] = jnp.where(replaced, placed, line_ref[:, window])

    cross = line_ref[:, :cols].astype(BF16)
    for chip in range(out_ref.shape[0]):
        out_ref[chip] = cross


def insert(meta, cross, slabs, width, chips):
    lines, cols = cross.shape
    return pl.pallas_call(
        functools.partial(insert_kernel, width),
        in_specs=[SMEM] + [VMEM] * 2,
        out_specs=VMEM,
        out_shape=jax.ShapeDtypeStruct((chips, lines, cols), BF16),
        scratch_shapes=[pltpu.VMEM((lines, cols + 128), F32)],
        compiler_params=pltpu.CompilerParams(vmem_limit_bytes=40 * 2**20),
        name="insert",
    )(meta, cross, slabs)


def sublane(value, row):
    return jnp.broadcast_to(value[row : row + 1, :], value.shape)


def lane(value, col):
    return jnp.broadcast_to(value[:, col : col + 1], value.shape)


def inverse_factor(matrix):
    size = matrix.shape[0]
    groups = size // 8
    cols = lax.broadcasted_iota(jnp.int32, (8, size), 1)
    rows = lax.broadcasted_iota(jnp.int32, (8, size), 0)
    a = [matrix[8 * g : 8 * g + 8, :] for g in range(groups)]
    m = [jnp.where(cols == rows + 8 * g, 1.0, 0.0).astype(F32) for g in range(groups)]
    for g in range(groups):
        pivot = [lane(a[g], 8 * g + c) for c in range(8)]
        below = {h: [lane(a[h], 8 * g + c) for c in range(8)] for h in range(g + 1, groups)}
        for c in range(8):
            reciprocal = 1.0 / sublane(pivot[c], c)
            a_row, m_row = sublane(a[g], c), sublane(m[g], c)
            pivots = [sublane(pivot[k], c) for k in range(8)]
            if c < 7:
                factor = jnp.where(rows > c, pivot[c] * reciprocal, 0.0)
                a[g] = a[g] - factor * a_row
                m[g] = m[g] - factor * m_row
                for k in range(c + 1, 8):
                    pivot[k] = pivot[k] - factor * pivots[k]
            for h in range(g + 1, groups):
                factor = below[h][c] * reciprocal
                a[h] = a[h] - factor * a_row
                m[h] = m[h] - factor * m_row
                for k in range(c + 1, 8):
                    below[h][k] = below[h][k] - factor * pivots[k]
    out = []
    for g in range(groups):
        diagonal = jnp.sum(jnp.where(cols == rows + 8 * g, a[g], 0.0), axis=1, keepdims=True)
        out.append(m[g] * lax.rsqrt(diagonal))
    return jnp.concatenate(out, axis=0)


def factor_kernel(row_total, meta, mine_ref, other_ref, out_ref, gram_ref):
    half = out_ref.shape[0] // 2
    eighth = half // 4
    gram_ref[meta[1]] = mine_ref[...]
    gram_ref[1 - meta[1]] = other_ref[...]
    gram = gram_ref[...] * (1.0 / row_total)
    unpack = lambda rows: jnp.concatenate([rows[:, :half], rows[:, half:]], axis=0)
    lower = jnp.concatenate([unpack(gram[0, 2 * eighth :]), unpack(gram[1, 2 * eighth :])], axis=0)
    first = inverse_factor(unpack(gram[0, : 2 * eighth]))
    upper = contract(first, lower, 1, 1, HIGHEST)
    rest = unpack(gram[1, : 2 * eighth]) - contract(upper, upper, 0, 0, HIGHEST)
    below = -contract(upper, first, 0, 0, HIGHEST)
    second = inverse_factor(rest)
    out_ref[:half, :half] = first
    out_ref[:half, half:] = jnp.zeros((half, half), F32)
    out_ref[half:, :half] = contract(second, below, 1, 0, HIGHEST)
    out_ref[half:, half:] = second


def invert(meta, mine, other, row_total):
    rank = mine.shape[1]
    return pl.pallas_call(
        functools.partial(factor_kernel, row_total),
        in_specs=[SMEM, VMEM, VMEM],
        out_specs=VMEM,
        out_shape=jax.ShapeDtypeStruct((rank, rank), F32),
        scratch_shapes=[pltpu.VMEM((CORES, *mine.shape), F32)],
        compiler_params=pltpu.CompilerParams(vmem_limit_bytes=40 * 2**20),
        name="invert",
    )(meta, mine, other)


def basis_kernel(inverse_ref, sketch_ref, out_ref):
    high, low = split(inverse_ref[...])
    sketch = sketch_ref[...]
    out_ref[...] = (contract(sketch, high, 1, 1) + contract(sketch, low, 1, 1)).astype(BF16)


def basis(inverse, sketch):
    return pl.pallas_call(
        basis_kernel,
        in_specs=[VMEM] * 2,
        out_specs=VMEM,
        out_shape=jax.ShapeDtypeStruct(sketch.shape, BF16),
        compiler_params=pltpu.CompilerParams(vmem_limit_bytes=40 * 2**20),
        name="basis",
    )(inverse, sketch)


def coefs_kernel(scale, meta, inverse_ref, mine_ref, other_ref, out_ref, cross_ref):
    half, _ = mine_ref.shape
    for ref, core in ((mine_ref, meta[1]), (other_ref, 1 - meta[1])):
        cross_ref[pl.ds(pl.multiple_of(core * half, half), half), :] = ref[...]
    high, low = split(inverse_ref[...] * scale)
    cross = cross_ref[...]
    out_ref[...] = contract(high, cross, 1, 0) + contract(low, cross, 1, 0)


def coefs(meta, inverse, mine, other, scale):
    rank, cols = inverse.shape[0], mine.shape[1]
    return pl.pallas_call(
        functools.partial(coefs_kernel, scale),
        in_specs=[SMEM] + [VMEM] * 3,
        out_specs=VMEM,
        out_shape=jax.ShapeDtypeStruct((rank, cols), F32),
        scratch_shapes=[pltpu.VMEM((rank, cols), BF16)],
        compiler_params=pltpu.CompilerParams(vmem_limit_bytes=40 * 2**20),
        name="coefs",
    )(meta, inverse, mine, other)


def exchange(value, axis, groups=None):
    return lax.all_to_all(value, axis, 0, 0, axis_index_groups=groups, tiled=True)


def local(window_values, window_scales, slab_values, slab_scales, test_matrix, owner_slot, offset):
    rows, cols = window_values.shape
    rank = test_matrix.shape[1]
    width = slab_values.shape[1]
    slots, spaces = lax.axis_size("slot"), lax.axis_size("space")
    chips = spaces // CORES
    same_core = [[CORES * i + c for i in range(chips)] for c in range(CORES)]
    row_total = rows * spaces
    slot, core = lax.axis_index("slot"), lax.rem(lax.axis_index("space"), CORES)
    owner, first = owner_slot[0], offset[0]
    where = jnp.arange(4)
    meta = jnp.where(
        where == 0,
        slot,
        jnp.where(
            where == 1,
            core,
            jnp.where(where == 2, jnp.where(slot == owner, first, 2 * cols), owner),
        ),
    ).astype(jnp.int32)

    test_rows = lax.dynamic_slice_in_dim(test_matrix, first, SLAB, 0)
    tests = lax.all_to_all(test_rows.reshape(slots, width, rank), "slot", 0, 0, tiled=True)
    window_values = pltpu.with_memory_space_constraint(window_values, pltpu.VMEM)
    partial = sketch_window(meta, window_values, window_scales, test_matrix)
    slab, slab_scale = slab_values.T, slab_scales.T
    x0, x1, x2, x3, x4a, x4b, x5, x6, x7 = add_slab(
        meta, partial, slab, slab_scale, tests, slots
    )

    right3, left3 = ring(x3, 1, slots), ring(x5, -1, slots)
    right4, left4 = ring(x4a, 2, slots), ring(x4b, -2, slots)
    right1, left1 = ring(x1, 1, slots), ring(x7, -1, slots)
    upper = x4a.shape[0]
    wide = lambda x: x.astype(F32)
    to_right = wide(x2) + wide(right3) + jnp.pad(wide(right4), ((0, upper), (0, 0)))
    to_left = wide(x6) + wide(left3) + jnp.pad(wide(left4), ((upper, 0), (0, 0)))
    right2, left2 = ring(to_right.astype(BF16), 2, slots), ring(to_left.astype(BF16), -2, slots)
    own = (wide(x0) + wide(right1) + wide(left1) + wide(right2) + wide(left2)).astype(BF16)

    right2, left2 = ring(own, 2, slots), ring(own, -2, slots)
    right1, left1 = ring(own, 1, slots), ring(own, -1, slots)
    right3, left3 = ring(right2, 1, slots), ring(left2, -1, slots)
    right4, left4 = ring(right2[:upper], 2, slots), ring(left2[upper:], -2, slots)
    sketch_blocks = [own, left1, left2, left3, right4, left4, right3, right2, right1]

    mine, theirs, gram_mine, gram_theirs, sketch = products(
        meta, window_values, window_scales, slab, slab_scale, sketch_blocks, slots
    )

    half = add_pair(mine, along(theirs, 0, 0, 1), chips)
    pieces = exchange(half, "space", same_core)
    total, new = sum_pieces(pieces, cols, slots)
    slabs = exchange(new, "slot")
    whole = insert(meta, total, slabs, width, chips)
    cross_mine = exchange(whole, "space", same_core)
    cross_mine = cross_mine.reshape(rank // CORES, cols)
    cross_other = along(cross_mine, 0, 0, 1)

    gram = gram_mine + along(gram_theirs, 0, 0, 1)
    for dy, dx in ((0, 1), (1, 0)):
        far, near, back = (along(gram, dy * d, dx * d) for d in (2, 1, 3))
        gram = (gram + far) + (near + back)
    gram_other = along(gram, 0, 0, 1)

    inverse = invert(meta, gram, gram_other, row_total)
    pod_basis = basis(inverse, sketch)
    pod_coefs = coefs(meta, inverse, cross_mine, cross_other, 1.0 / float(row_total) ** 0.5)
    return pod_basis, pod_coefs


def solution(mesh):
    return jax.shard_map(
        local,
        mesh=mesh,
        in_specs=(
            P("space", "slot"),
            P("space", "slot"),
            P("space", "slot"),
            P("space", "slot"),
            P("slot", None),
            P(),
            P(),
        ),
        out_specs=(P("space", None), P(None, "slot")),
        check_vma=False,
    )
```

```python
import functools

import jax
import jax.numpy as jnp
from jax import lax
from jax.experimental import pallas as pl
from jax.experimental.pallas import tpu as pltpu
from jax.sharding import PartitionSpec as P


SLAB = 512
BLOCK = 128
F32, BF16 = jnp.float32, jnp.bfloat16
HIGHEST = lax.Precision.HIGHEST

CORES = 2
CHUNKS = 4


def space_shift(dy, dx, dc=0):
    index = lambda y, x, c: (y % 4) * 8 + (x % 4) * 2 + c
    return [
        (index(y, x, c), index(y + dy, x + dx, (c + dc) % 2))
        for y in range(4)
        for x in range(4)
        for c in range(2)
    ]


def ring(value, distance, size):
    return lax.ppermute(value, "slot", [(i, (i + distance) % size) for i in range(size)])


def along(value, dy, dx, dc=0):
    return lax.ppermute(value, "space", space_shift(dy, dx, dc))


def contract(left, right, left_dim, right_dim, precision=None):
    return lax.dot_general(
        left,
        right,
        (((left_dim,), (right_dim,)), ((), ())),
        precision=precision,
        preferred_element_type=F32,
    )


def split(value):
    high = value.astype(BF16)
    return high, (value - high.astype(F32)).astype(BF16)


VMEM = pl.BlockSpec(memory_space=pltpu.VMEM)
SMEM = pl.BlockSpec(memory_space=pltpu.SMEM)


def expand(values_ref, scale_ref, first, count):
    return jnp.concatenate(
        [
            values_ref[BLOCK * b : BLOCK * (b + 1), :] * scale_ref[b : b + 1, :].astype(BF16)
            for b in range(first, first + count)
        ],
        axis=0,
    )


def expand_slab(slab_ref, scale_ref, row_blocks):
    return jnp.concatenate(
        [
            slab_ref[:, BLOCK * b : BLOCK * (b + 1)] * scale_ref[:, b : b + 1].astype(BF16)
            for b in range(row_blocks)
        ],
        axis=1,
    )


def sketch_kernel(meta, values_ref, scales_ref, test_ref, out_ref, scale_ref):
    columns = lax.broadcasted_iota(jnp.int32, scales_ref.shape, 1)
    evicted = (columns >= meta[2]) & (columns < meta[2] + SLAB)
    scale_ref[...] = jnp.where(evicted, 0.0, scales_ref[...].astype(F32))
    row_blocks = scales_ref.shape[0]
    count = row_blocks // 4
    for first in range(0, row_blocks, count):
        window = expand(values_ref, scale_ref, first, count)
        out_ref[BLOCK * first : BLOCK * (first + count), :] = jnp.dot(
            window, test_ref[...], preferred_element_type=F32
        )


def sketch_window(meta, values, scales, test):
    return pl.pallas_call(
        sketch_kernel,
        in_specs=[SMEM] + [VMEM] * 3,
        out_specs=VMEM,
        out_shape=jax.ShapeDtypeStruct((values.shape[0], test.shape[1]), F32),
        scratch_shapes=[pltpu.VMEM(scales.shape, F32)],
        compiler_params=pltpu.CompilerParams(vmem_limit_bytes=40 * 2**20),
        name="sketch_window",
    )(meta, values, scales, test)


def slab_kernel(parts, meta, partial_ref, slab_ref, scales_ref, tests_ref, *refs):
    out_refs, sum_ref, scale_ref = refs[:-2], refs[-2], refs[-1]
    rows = partial_ref.shape[0] // parts
    scale_ref[...] = scales_ref[...].astype(F32)
    slab = expand_slab(slab_ref, scale_ref, partial_ref.shape[0] // BLOCK)
    sum_ref[...] = (partial_ref[...] + contract(slab, tests_ref[meta[3]], 0, 0)).astype(BF16)
    pieces = []
    for k in range(parts):
        whole = (k, 0, rows)
        pieces += [(k, 0, rows // 2), (k, rows // 2, rows)] if 2 * k == parts else [whole]
    for out_ref, (k, start, stop) in zip(out_refs, pieces):
        block = pl.multiple_of(lax.rem(meta[0] + k, parts) * rows + start, rows // 2)
        out_ref[...] = sum_ref[pl.ds(block, stop - start), :]


def add_slab(meta, partial, slab, scales, tests, parts):
    rows, rank = partial.shape
    sizes = [rows // parts] * (parts // 2) + [rows // parts // 2] * 2
    sizes += [rows // parts] * (parts // 2 - 1)
    return pl.pallas_call(
        functools.partial(slab_kernel, parts),
        in_specs=[SMEM] + [VMEM] * 4,
        out_specs=[VMEM] * len(sizes),
        out_shape=[jax.ShapeDtypeStruct((size, rank), BF16) for size in sizes],
        scratch_shapes=[pltpu.VMEM(partial.shape, BF16), pltpu.VMEM(scales.shape, F32)],
        compiler_params=pltpu.CompilerParams(vmem_limit_bytes=40 * 2**20),
        name="add_slab",
    )(meta, partial, slab, scales, tests)


def gather_blocks(parts, meta, sketch_refs, out_ref):
    rows = out_ref.shape[0] // parts
    start = 0
    for ref in sketch_refs:
        k, inside = divmod(start, rows)
        line = pl.multiple_of(lax.rem(meta[0] + k, parts) * rows + inside, rows // 2)
        out_ref[pl.ds(line, ref.shape[0]), :] = ref[...]
        start += ref.shape[0]


def cross_kernel(parts, meta, values_ref, scales_ref, slab_ref, slab_scales_ref, *refs):
    sketch_refs, refs = refs[:-11], refs[-11:]
    mine_ref, theirs_ref, gram_mine_ref, gram_theirs_ref, sketch_ref = refs[:5]
    cross_ref, gram_ref, scale_ref, slab_scale_ref = refs[5:9]
    window_ref, arrived = refs[9:]
    chunk = values_ref.shape[0] // CHUNKS
    copies = []
    for i in range(CHUNKS):
        lines = pl.ds(chunk * i, chunk)
        copies.append(
            pltpu.make_async_copy(values_ref.at[lines, :], window_ref.at[lines, :], arrived.at[i])
        )
        copies[-1].start()
    gather_blocks(parts, meta, sketch_refs, sketch_ref)
    scale_ref[...] = scales_ref[...].astype(F32)
    slab_scale_ref[...] = slab_scales_ref[...].astype(F32)
    rank, row_blocks = sketch_ref.shape[1], scales_ref.shape[0]
    width, cols = slab_ref.shape[0], values_ref.shape[1]
    sketch = sketch_ref[...]
    gram = contract(sketch, sketch, 0, 0)
    half, eighth = rank // 2, rank // 8
    for c in range(CORES):
        block = gram[half * c : half * (c + 1), half * c : half * (c + 1)]
        below = gram[half + 2 * eighth * c : half + 2 * eighth * (c + 1), :half]
        gram_ref[c, : half // 2, :half] = block[: half // 2]
        gram_ref[c, : half // 2, half:] = block[half // 2 :]
        gram_ref[c, half // 2 :, :half] = below[:eighth]
        gram_ref[c, half // 2 :, half:] = below[eighth:]
    slab = expand_slab(slab_ref, slab_scale_ref, row_blocks)
    cross_ref[:, cols:] = jnp.zeros((rank, cross_ref.shape[1] - cols), F32)
    cross_ref[:, cols : cols + width] = contract(sketch, slab, 0, 1)
    count = row_blocks // CHUNKS
    for first in range(0, row_blocks, count):
        copies[first // count].wait()
        window = expand(window_ref, scale_ref, first, count)
        part = contract(sketch[BLOCK * first : BLOCK * (first + count), :], window, 0, 0)
        cross_ref[:, :cols] = part if first == 0 else cross_ref[:, :cols] + part
    core = meta[1]
    for out, gram_out, which in (
        (mine_ref, gram_mine_ref, core),
        (theirs_ref, gram_theirs_ref, 1 - core),
    ):
        lines = pl.ds(pl.multiple_of(which * half, half), half)
        out[...] = cross_ref[lines, :].astype(BF16)
        gram_out[...] = gram_ref[which]


def products(meta, values, scales, slab, slab_scales, sketch_blocks, parts):
    rows, cols = values.shape
    rank = sketch_blocks[0].shape[1]
    half, lanes = rank // CORES, cols + 128
    gram_half = (3 * rank // 8, rank)
    return pl.pallas_call(
        functools.partial(cross_kernel, parts),
        in_specs=[SMEM, pl.BlockSpec(memory_space=pltpu.HBM)] + [VMEM] * (3 + len(sketch_blocks)),
        out_specs=[VMEM] * 5,
        out_shape=[jax.ShapeDtypeStruct((half, lanes), BF16)] * 2
        + [jax.ShapeDtypeStruct(gram_half, F32)] * 2
        + [jax.ShapeDtypeStruct((rows, rank), BF16)],
        scratch_shapes=[
            pltpu.VMEM((rank, lanes), F32),
            pltpu.VMEM((CORES, *gram_half), F32),
            pltpu.VMEM(scales.shape, F32),
            pltpu.VMEM(slab_scales.shape, F32),
            pltpu.VMEM(values.shape, BF16),
            pltpu.SemaphoreType.DMA((CHUNKS,)),
        ],
        compiler_params=pltpu.CompilerParams(vmem_limit_bytes=40 * 2**20),
        name="products",
    )(meta, values, scales, slab, slab_scales, *sketch_blocks)


def pair_kernel(mine_ref, other_ref, out_ref):
    lines = out_ref.shape[1]
    total = mine_ref[...].astype(F32) + other_ref[...].astype(F32)
    for chip in range(out_ref.shape[0]):
        out_ref[chip] = total[lines * chip : lines * (chip + 1), :].astype(BF16)


def add_pair(mine, other, chips):
    rows, lanes = mine.shape
    return pl.pallas_call(
        pair_kernel,
        in_specs=[VMEM] * 2,
        out_specs=VMEM,
        out_shape=jax.ShapeDtypeStruct((chips, rows // chips, lanes), BF16),
        compiler_params=pltpu.CompilerParams(vmem_limit_bytes=40 * 2**20),
        name="add_pair",
    )(mine, other)


def sum_kernel(pieces_ref, cross_ref, new_ref):
    cols = cross_ref.shape[1]
    total = pieces_ref[0].astype(F32)
    for chip in range(1, pieces_ref.shape[0]):
        total += pieces_ref[chip].astype(F32)
    cross_ref[...] = total[:, :cols]
    new = total[:, cols:].astype(BF16)
    for slot in range(new_ref.shape[0]):
        new_ref[slot] = new


def sum_pieces(pieces, cols, slots):
    _, lines, lanes = pieces.shape
    return pl.pallas_call(
        sum_kernel,
        in_specs=[VMEM],
        out_specs=[VMEM] * 2,
        out_shape=[
            jax.ShapeDtypeStruct((lines, cols), F32),
            jax.ShapeDtypeStruct((slots, lines, lanes - cols), BF16),
        ],
        compiler_params=pltpu.CompilerParams(vmem_limit_bytes=40 * 2**20),
        name="sum_pieces",
    )(pieces)


def insert_kernel(width, meta, cross_ref, slabs_ref, out_ref, line_ref):
    lines, cols = cross_ref.shape
    line_ref[:, :cols] = cross_ref[...]

    @pl.when(meta[2] < cols)
    def _():
        slots, _, lanes = slabs_ref.shape
        inside = lax.rem(meta[2], 128)
        window = pl.ds(pl.multiple_of(meta[2] - inside, 128), SLAB + 128)
        column = lax.broadcasted_iota(jnp.int32, (lanes, SLAB + 128), 1)
        row = lax.broadcasted_iota(jnp.int32, (lanes, SLAB + 128), 0)
        placed = jnp.zeros((lines, SLAB + 128), F32)
        for slot in range(slots):
            hit = (column == row + (inside + width * slot)) & (row < width)
            selection = jnp.where(hit, 1.0, 0.0).astype(BF16)
            placed += contract(slabs_ref[slot], selection, 1, 0)
        column = lax.broadcasted_iota(jnp.int32, placed.shape, 1)
        replaced = (column >= inside) & (column < inside + SLAB)
        line_ref[:, window] = jnp.where(replaced, placed, line_ref[:, window])

    cross = line_ref[:, :cols].astype(BF16)
    for chip in range(out_ref.shape[0]):
        out_ref[chip] = cross


def insert(meta, cross, slabs, width, chips):
    lines, cols = cross.shape
    return pl.pallas_call(
        functools.partial(insert_kernel, width),
        in_specs=[SMEM] + [VMEM] * 2,
        out_specs=VMEM,
        out_shape=jax.ShapeDtypeStruct((chips, lines, cols), BF16),
        scratch_shapes=[pltpu.VMEM((lines, cols + 128), F32)],
        compiler_params=pltpu.CompilerParams(vmem_limit_bytes=40 * 2**20),
        name="insert",
    )(meta, cross, slabs)


def sublane(value, row):
    return jnp.broadcast_to(value[row : row + 1, :], value.shape)


def lane(value, col):
    return jnp.broadcast_to(value[:, col : col + 1], value.shape)


def inverse_factor(matrix):
    size = matrix.shape[0]
    groups = size // 8
    cols = lax.broadcasted_iota(jnp.int32, (8, size), 1)
    rows = lax.broadcasted_iota(jnp.int32, (8, size), 0)
    a = [matrix[8 * g : 8 * g + 8, :] for g in range(groups)]
    m = [jnp.where(cols == rows + 8 * g, 1.0, 0.0).astype(F32) for g in range(groups)]
    for g in range(groups):
        pivot = [lane(a[g], 8 * g + c) for c in range(8)]
        below = {h: [lane(a[h], 8 * g + c) for c in range(8)] for h in range(g + 1, groups)}
        for c in range(8):
            reciprocal = 1.0 / sublane(pivot[c], c)
            a_row, m_row = sublane(a[g], c), sublane(m[g], c)
            pivots = [sublane(pivot[k], c) for k in range(8)]
            if c < 7:
                factor = jnp.where(rows > c, pivot[c] * reciprocal, 0.0)
                a[g] = a[g] - factor * a_row
                m[g] = m[g] - factor * m_row
                for k in range(c + 1, 8):
                    pivot[k] = pivot[k] - factor * pivots[k]
            for h in range(g + 1, groups):
                factor = below[h][c] * reciprocal
                a[h] = a[h] - factor * a_row
                m[h] = m[h] - factor * m_row
                for k in range(c + 1, 8):
                    below[h][k] = below[h][k] - factor * pivots[k]
    out = []
    for g in range(groups):
        diagonal = jnp.sum(jnp.where(cols == rows + 8 * g, a[g], 0.0), axis=1, keepdims=True)
        out.append(m[g] * lax.rsqrt(diagonal))
    return jnp.concatenate(out, axis=0)


def factor_kernel(row_total, meta, mine_ref, other_ref, out_ref, gram_ref):
    half = out_ref.shape[0] // 2
    eighth = half // 4
    gram_ref[meta[1]] = mine_ref[...]
    gram_ref[1 - meta[1]] = other_ref[...]
    gram = gram_ref[...] * (1.0 / row_total)
    unpack = lambda rows: jnp.concatenate([rows[:, :half], rows[:, half:]], axis=0)
    lower = jnp.concatenate([unpack(gram[0, 2 * eighth :]), unpack(gram[1, 2 * eighth :])], axis=0)
    first = inverse_factor(unpack(gram[0, : 2 * eighth]))
    upper = contract(first, lower, 1, 1, HIGHEST)
    rest = unpack(gram[1, : 2 * eighth]) - contract(upper, upper, 0, 0, HIGHEST)
    below = -contract(upper, first, 0, 0, HIGHEST)
    second = inverse_factor(rest)
    out_ref[:half, :half] = first
    out_ref[:half, half:] = jnp.zeros((half, half), F32)
    out_ref[half:, :half] = contract(second, below, 1, 0, HIGHEST)
    out_ref[half:, half:] = second


def invert(meta, mine, other, row_total):
    rank = mine.shape[1]
    return pl.pallas_call(
        functools.partial(factor_kernel, row_total),
        in_specs=[SMEM, VMEM, VMEM],
        out_specs=VMEM,
        out_shape=jax.ShapeDtypeStruct((rank, rank), F32),
        scratch_shapes=[pltpu.VMEM((CORES, *mine.shape), F32)],
        compiler_params=pltpu.CompilerParams(vmem_limit_bytes=40 * 2**20),
        name="invert",
    )(meta, mine, other)


def basis_kernel(inverse_ref, sketch_ref, out_ref):
    high, low = split(inverse_ref[...])
    sketch = sketch_ref[...]
    out_ref[...] = (contract(sketch, high, 1, 1) + contract(sketch, low, 1, 1)).astype(BF16)


def basis(inverse, sketch):
    return pl.pallas_call(
        basis_kernel,
        in_specs=[VMEM] * 2,
        out_specs=VMEM,
        out_shape=jax.ShapeDtypeStruct(sketch.shape, BF16),
        compiler_params=pltpu.CompilerParams(vmem_limit_bytes=40 * 2**20),
        name="basis",
    )(inverse, sketch)


def coefs_kernel(scale, meta, inverse_ref, mine_ref, other_ref, out_ref, cross_ref):
    half, _ = mine_ref.shape
    for ref, core in ((mine_ref, meta[1]), (other_ref, 1 - meta[1])):
        cross_ref[pl.ds(pl.multiple_of(core * half, half), half), :] = ref[...]
    high, low = split(inverse_ref[...] * scale)
    cross = cross_ref[...]
    out_ref[...] = contract(high, cross, 1, 0) + contract(low, cross, 1, 0)


def coefs(meta, inverse, mine, other, scale):
    rank, cols = inverse.shape[0], mine.shape[1]
    return pl.pallas_call(
        functools.partial(coefs_kernel, scale),
        in_specs=[SMEM] + [VMEM] * 3,
        out_specs=VMEM,
        out_shape=jax.ShapeDtypeStruct((rank, cols), F32),
        scratch_shapes=[pltpu.VMEM((rank, cols), BF16)],
        compiler_params=pltpu.CompilerParams(vmem_limit_bytes=40 * 2**20),
        name="coefs",
    )(meta, inverse, mine, other)


def exchange(value, axis, groups=None):
    return lax.all_to_all(value, axis, 0, 0, axis_index_groups=groups, tiled=True)


def local(window_values, window_scales, slab_values, slab_scales, test_matrix, owner_slot, offset):
    rows, cols = window_values.shape
    rank = test_matrix.shape[1]
    width = slab_values.shape[1]
    slots, spaces = lax.axis_size("slot"), lax.axis_size("space")
    chips = spaces // CORES
    same_core = [[CORES * i + c for i in range(chips)] for c in range(CORES)]
    row_total = rows * spaces
    slot, core = lax.axis_index("slot"), lax.rem(lax.axis_index("space"), CORES)
    owner, first = owner_slot[0], offset[0]
    where = jnp.arange(4)
    meta = jnp.where(
        where == 0,
        slot,
        jnp.where(
            where == 1,
            core,
            jnp.where(where == 2, jnp.where(slot == owner, first, 2 * cols), owner),
        ),
    ).astype(jnp.int32)

    test_rows = lax.dynamic_slice_in_dim(test_matrix, first, SLAB, 0)
    tests = lax.all_to_all(test_rows.reshape(slots, width, rank), "slot", 0, 0, tiled=True)
    resident = pltpu.with_memory_space_constraint(window_values, pltpu.VMEM)
    partial = sketch_window(meta, resident, window_scales, test_matrix)
    slab, slab_scale = slab_values.T, slab_scales.T
    x0, x1, x2, x3, x4a, x4b, x5, x6, x7 = add_slab(
        meta, partial, slab, slab_scale, tests, slots
    )

    right3, left3 = ring(x3, 1, slots), ring(x5, -1, slots)
    right4, left4 = ring(x4a, 2, slots), ring(x4b, -2, slots)
    right1, left1 = ring(x1, 1, slots), ring(x7, -1, slots)
    upper = x4a.shape[0]
    wide = lambda x: x.astype(F32)
    to_right = wide(x2) + wide(right3) + jnp.pad(wide(right4), ((0, upper), (0, 0)))
    to_left = wide(x6) + wide(left3) + jnp.pad(wide(left4), ((upper, 0), (0, 0)))
    right2, left2 = ring(to_right.astype(BF16), 2, slots), ring(to_left.astype(BF16), -2, slots)
    own = (wide(x0) + wide(right1) + wide(left1) + wide(right2) + wide(left2)).astype(BF16)

    right2, left2 = ring(own, 2, slots), ring(own, -2, slots)
    right1, left1 = ring(own, 1, slots), ring(own, -1, slots)
    right3, left3 = ring(right2, 1, slots), ring(left2, -1, slots)
    right4, left4 = ring(right2[:upper], 2, slots), ring(left2[upper:], -2, slots)
    sketch_blocks = [own, left1, left2, left3, right4, left4, right3, right2, right1]

    mine, theirs, gram_mine, gram_theirs, sketch = products(
        meta, window_values, window_scales, slab, slab_scale, sketch_blocks, slots
    )

    half = add_pair(mine, along(theirs, 0, 0, 1), chips)
    pieces = exchange(half, "space", same_core)
    total, new = sum_pieces(pieces, cols, slots)
    slabs = exchange(new, "slot")
    whole = insert(meta, total, slabs, width, chips)
    cross_mine = exchange(whole, "space", same_core)
    cross_mine = cross_mine.reshape(rank // CORES, cols)
    cross_other = along(cross_mine, 0, 0, 1)

    gram = gram_mine + along(gram_theirs, 0, 0, 1)
    for dy, dx in ((0, 1), (1, 0)):
        far, near, back = (along(gram, dy * d, dx * d) for d in (2, 1, 3))
        gram = (gram + far) + (near + back)
    gram_other = along(gram, 0, 0, 1)

    inverse = invert(meta, gram, gram_other, row_total)
    pod_basis = basis(inverse, sketch)
    pod_coefs = coefs(meta, inverse, cross_mine, cross_other, 1.0 / float(row_total) ** 0.5)
    return pod_basis, pod_coefs


def solution(mesh):
    return jax.shard_map(
        local,
        mesh=mesh,
        in_specs=(
            P("space", "slot"),
            P("space", "slot"),
            P("space", "slot"),
            P("space", "slot"),
            P("slot", None),
            P(),
            P(),
        ),
        out_specs=(P("space", None), P(None, "slot")),
        check_vma=False,
    )
```
